32 devices in a mesh: grp: 4 (over x, core), ep: 8 (over z, y).
Axes of the slice: x: 2, y: 2, z: 4, core: 2. Of those that a mesh axis runs over, the one named last changes fastest.
Arguments:
- features: bfloat16 [8192, 1152], P(('grp', 'ep')), may hold values from -6 to 6
- token_position: int32 [8192], P(('grp', 'ep')), may hold values from 0 to 2047, as said below
- expert_ids: int32 [8192, 2], P(('grp', 'ep')), may hold values from 0 to 7, all different within a row; in each aligned block of 256 rows (0 to 255, 256 to 511, ...) at most 128 rows name the same one
- proj_in: bfloat16 [1152, 2560], P('ep'), may hold values from -0.1875 to 0.1875
- bias_in: float32 [2560], replicated, may hold values from -3 to 3
- proj_out: bfloat16 [2560, 2560], P('ep'), may hold values from -0.125 to 0.125
- bias_out: float32 [2560], replicated, may hold values from -3 to 3
- norm_gain: float32 [2560], replicated, may hold values from 0.1 to 1.9
- router: bfloat16 [2560, 8], replicated, may hold values from -0.125 to 0.125
- w_gate: bfloat16 [8, 2560, 512], P('ep'), may hold values from -0.125 to 0.125
- w_up: bfloat16 [8, 2560, 512], P('ep'), may hold values from -0.125 to 0.125
- w_down: bfloat16 [8, 512, 2560], P('ep'), may hold values from -0.25 to 0.25
Outputs:
- mixed: bfloat16 [8192, 2560], P(('grp', 'ep'))
The draws below stay inside these ranges and needn't reach their ends.
Inputs may be any that keep to these rules, and one draw needn't show every extreme that they name: `token_position`: within each group of 8 devices along ep, the group's values form a permutation of 0 to 2047; position q belongs to the device of ep index q // 256. The rows of each device hold exactly 32 positions of every device of its group. `expert_ids`: each row names 2 different experts; no expert is named by more than 128 of the rows of one device.
All inputs are finite; a program needn't handle non-finite values.
Results may differ from the reference program's by a relative error of at most 0.0071.
Values may be sent and summed in bfloat16 or wider, within the bound.
A program may use at most 192 MiB of HBM per device.

```python
import math
import jax
import jax.numpy as jnp
import numpy as np
from jax import lax

D_VIS = 1152
D = 2560
FF_E = 512
TOP = 2
EXP_DEV = 1
ROWS = 256
EXPERTS = 8
CAP = 128
ROWS_ALL = 8192
N_GRP = 4
N_EP = 8


def group_positions(group_key):
    first_key, second_key = jax.random.split(group_key)
    per_peer = ROWS // N_EP
    template = jnp.repeat(jnp.arange(N_EP, dtype=jnp.int32), per_peer)

    def shuffle_template(single_key):
        return jax.random.permutation(single_key, template)

    def shuffle_rows(single_key):
        return jax.random.permutation(single_key, ROWS).astype(jnp.int32)
    destinations = jax.vmap(shuffle_template)(jax.random.split(first_key, N_EP))
    dest_hot = (destinations[:, :, None] == jnp.arange(N_EP, dtype=jnp.int32)[None, None, :]).astype(jnp.int32)
    ranking = jnp.sum((jnp.cumsum(dest_hot, axis=1) - 1) * dest_hot, axis=2)
    canonical = jnp.arange(N_EP, dtype=jnp.int32)[:, None] * per_peer + ranking
    shuffles = jax.vmap(shuffle_rows)(jax.random.split(second_key, N_EP))
    landing = shuffles[destinations, canonical]
    return (destinations * ROWS + landing).reshape(N_EP * ROWS).astype(jnp.int32)


def draw_token_position(key, part):
    group_keys = jax.random.split(jax.random.fold_in(key, 17), N_GRP)
    return jax.vmap(group_positions)(group_keys).reshape(N_GRP * N_EP * ROWS)


def shard_levels(rng, shape, pieces, smallest, top_value):
    def one(dim, blocks):
        heights = jax.random.uniform(jax.random.fold_in(jax.random.fold_in(rng, 6), dim), (blocks,), jnp.float32, smallest / len(pieces), top_value / len(pieces))
        return jnp.repeat(jnp.exp(heights), shape[dim] // blocks).reshape((-1,) + (1,) * (len(shape) - dim - 1))

    level = one(*pieces[0])
    for cut in pieces[1:]:
        level = level * one(*cut)
    return level


def deal_out(own_key, own, number, rows, number_of, top, bound, skew):
    sequence = jax.random.permutation(own_key, number_of)
    packed, common = load_shares(number_of, rows * top, bound, skew, True), load_shares(number_of, rows * top, bound, skew, False)
    places = jnp.arange(number_of)

    def named(tallies, offset_by):
        used = int((tallies > 0).sum())
        fixed = max(1, used // 4)
        moved = fixed + (places - fixed + offset_by * (used - fixed)) % max(1, number_of - fixed)
        return jnp.zeros((number_of,), jnp.int32).at[sequence[jnp.where(places < fixed, places, moved)]].set(jnp.asarray(tallies, jnp.int32))

    tallies = jnp.where(number % 4 == 0, named(packed, number // 4), named(common, number - number // 4 - 1))
    mixed = jax.random.permutation(jax.random.fold_in(own, 3), number_of)
    donor, taker = mixed[0:number_of // 2 * 2:2], mixed[1:number_of // 2 * 2:2]
    margin = jnp.minimum(tallies[donor] - 1, bound - tallies[taker]) // 2
    margin = jnp.where((donor == sequence[0]) | (taker == sequence[0]) | (tallies[taker] == 0), 0, jnp.maximum(margin, 0))
    moved = jax.random.randint(jax.random.fold_in(own, 4), (number_of // 2,), 0, 1 << 20) % (margin + 1)
    tallies = tallies.at[donor].add(-moved).at[taker].add(moved)
    labels = jnp.searchsorted(jnp.cumsum(tallies), jnp.arange(rows * top), side="right").astype(jnp.int32)
    grid = labels.reshape(top, rows).T
    grid = grid[jax.random.permutation(jax.random.fold_in(own, 1), rows)]
    offset_by = jax.random.randint(jax.random.fold_in(own, 2), (rows, 1), 0, top)
    return jnp.take_along_axis(grid, (jnp.arange(top)[None, :] + offset_by) % top, axis=1)


def load_shares(count, total, bound, slope, full):
    loads = [(1 << 20) // math.isqrt(rank ** slope) + 1 for rank in range(1, count + 1)]
    largest = bound if full else min(bound, max(-(-total // count), total * loads[0] // sum(loads)))
    least = 1 if total - largest >= count - 1 else 0
    counts, surplus = [largest] + [least] * (count - 1), total - largest - least * (count - 1)
    while surplus > 0:
        movable = [i for i in range(1, count) if counts[i] < largest] or [i for i in range(1, count) if counts[i] < bound]
        whole, left = sum([loads[i] for i in movable]), surplus
        for i in movable:
            addition = min(bound - counts[i], max(1, left * loads[i] // whole), surplus)
            counts[i] = counts[i] + addition
            surplus = surplus - addition
    return np.array(counts)


def centred(key, extent, spread, reach, cuts=(), kind=jnp.bfloat16):
    loudness = shard_levels(key, extent, cuts, -0.22, 0.18) if cuts else 1.0
    entries = jax.random.normal(key, extent, jnp.float32) * spread * loudness
    return jnp.minimum(jnp.maximum(entries, -reach), reach).astype(kind)


def setup_inputs(seed: int = 0) -> dict:
    arg_keys = jax.random.split(jax.random.key(seed), 13)
    features = centred(arg_keys[0], (ROWS_ALL, D_VIS), 1.0, 6.0, ((0, 32),))
    token_position = draw_token_position(jax.random.fold_in(arg_keys[12], 71), 0)
    expert_ids_keys = jax.random.split(jax.random.fold_in(arg_keys[2], 1), ROWS_ALL // ROWS)
    expert_ids_turns = jax.random.permutation(jax.random.fold_in(arg_keys[2], 3), ROWS_ALL // ROWS)
    expert_ids = jax.vmap(lambda own, number: deal_out(jax.random.fold_in(arg_keys[2], 2), own, number, ROWS, EXPERTS, TOP, CAP, 2))(expert_ids_keys, expert_ids_turns).reshape((ROWS_ALL, TOP))
    proj_in = centred(arg_keys[3], (D_VIS, D), D_VIS ** -0.5, 0.1875, ((0, 8),))
    bias_in = centred(arg_keys[4], (D,), 0.5, 3.0, (), jnp.float32)
    proj_out = centred(arg_keys[5], (D, D), D ** -0.5, 0.125, ((0, 8),))
    bias_out = centred(arg_keys[6], (D,), 0.5, 3.0, (), jnp.float32)
    norm_gain = jnp.clip(1.0 + 0.18 * jax.random.normal(arg_keys[7], (D,), jnp.float32), 0.1, 1.9)
    router = centred(arg_keys[8], (D, EXPERTS), D ** -0.5, 0.125)
    w_gate = centred(arg_keys[9], (EXPERTS, D, FF_E), D ** -0.5, 0.125, ((0, 8),))
    w_up = centred(arg_keys[10], (EXPERTS, D, FF_E), D ** -0.5, 0.125, ((0, 8),))
    w_down = centred(arg_keys[11], (EXPERTS, FF_E, D), FF_E ** -0.5, 0.25, ((0, 8),))
    return {"features": features, "token_position": token_position, "expert_ids": expert_ids, "proj_in": proj_in, "bias_in": bias_in, "proj_out": proj_out, "bias_out": bias_out, "norm_gain": norm_gain, "router": router, "w_gate": w_gate, "w_up": w_up, "w_down": w_down}


EPSILON = 1e-06

def run_expert(operands):
    rows_in, gate_weight, up_weight, down_weight = operands
    gate_part = jnp.dot(rows_in, gate_weight, preferred_element_type=jnp.float32)
    up_part = jnp.dot(rows_in, up_weight, preferred_element_type=jnp.float32)
    activated = (jax.nn.silu(gate_part) * up_part).astype(jnp.bfloat16)
    return jnp.dot(activated, down_weight, preferred_element_type=jnp.float32).astype(jnp.bfloat16)

def reference(features, token_position, expert_ids, proj_in, bias_in, proj_out, bias_out, norm_gain, router, w_gate, w_up, w_down):
    group_rows = N_EP * ROWS
    experts = EXP_DEV * N_EP
    capacity = 2 * ROWS * TOP // experts

    def one_group(group_index):
        offset = (group_index * group_rows).astype(jnp.int32)
        patches = lax.dynamic_slice_in_dim(features, offset, group_rows, 0)
        positions = lax.dynamic_slice_in_dim(token_position, offset, group_rows, 0)
        choices = lax.dynamic_slice_in_dim(expert_ids, offset, group_rows, 0)
        pre_act = jnp.dot(patches, proj_in, preferred_element_type=jnp.float32) + bias_in
        hidden = jax.nn.gelu(pre_act, approximate=False).astype(jnp.bfloat16)
        projected = (jnp.dot(hidden, proj_out, preferred_element_type=jnp.float32) + bias_out).astype(jnp.bfloat16)
        tokens = jnp.zeros_like(projected).at[positions].set(projected)
        wide = tokens.astype(jnp.float32)
        scale = lax.rsqrt(lax.optimization_barrier(jnp.mean(wide * wide, axis=-1, keepdims=True)) + EPSILON)
        normed = (wide * scale * norm_gain).astype(jnp.bfloat16)
        logits = jnp.dot(normed, router, preferred_element_type=jnp.float32)
        chosen_mask = choices[:, :, None] == jnp.arange(experts, dtype=jnp.int32)[None, None, :]
        chosen = lax.optimization_barrier(jnp.sum(jnp.where(chosen_mask, logits[:, None, :], 0.0), axis=2))
        first_gate = jax.nn.sigmoid(chosen[:, 0] - chosen[:, 1])
        gates = jnp.stack([first_gate, 1.0 - first_gate], axis=1)
        pair_expert = choices.reshape(N_EP, ROWS * TOP)
        pair_hot = (pair_expert[:, :, None] == jnp.arange(experts, dtype=jnp.int32)[None, None, :]).astype(jnp.int32)
        pair_slot = lax.optimization_barrier(jnp.sum((jnp.cumsum(pair_hot, axis=1) - 1) * pair_hot, axis=2)).astype(jnp.int32)
        device_index = jnp.broadcast_to(jnp.arange(N_EP, dtype=jnp.int32)[:, None], (N_EP, ROWS * TOP))
        pair_rows = jnp.repeat(normed, TOP, axis=0).reshape(N_EP, ROWS * TOP, D)
        blocks = jnp.zeros((experts, N_EP, capacity, D), jnp.bfloat16).at[pair_expert, device_index, pair_slot].set(pair_rows)
        outputs = lax.map(run_expert, (blocks.reshape(experts, N_EP * capacity, D), w_gate, w_up, w_down))
        outputs = outputs.reshape(experts, N_EP, capacity, D)
        combined = outputs[pair_expert, device_index, pair_slot].reshape(group_rows, TOP, D)
        total = wide + lax.optimization_barrier(jnp.sum(gates[:, :, None] * combined.astype(jnp.float32), axis=1))
        return total.astype(jnp.bfloat16)
    results = lax.map(one_group, jnp.arange(N_GRP, dtype=jnp.int32))
    return results.reshape(N_GRP * group_rows, D)
```

```python
import jax
import jax.numpy as jnp
from jax import lax
from jax.sharding import PartitionSpec as P

EPSILON = 1e-06
F32 = jnp.float32
BF16 = jnp.bfloat16


def select_rows(mask, rows):
    return jnp.dot(mask.astype(BF16), rows, preferred_element_type=F32).astype(BF16)


def gather_columns(weight):
    members = lax.axis_size("grp")
    width = weight.shape[1] // members
    part = lax.dynamic_slice_in_dim(weight, lax.axis_index("grp") * width, width, 1)
    full = lax.all_gather(part, ("grp", "ep"), axis=0, tiled=True)
    return full.reshape(members, -1, width)


def shards(
    features,
    token_position,
    expert_ids,
    proj_in,
    bias_in,
    proj_out,
    bias_out,
    norm_gain,
    router,
    w_gate,
    w_up,
    w_down,
):
    members = lax.axis_size("ep")
    row_count, vis = features.shape
    width = proj_in.shape[1]
    first_full = gather_columns(proj_in)
    second_full = gather_columns(proj_out)

    index = jnp.arange(row_count, dtype=jnp.int32)
    rank = jnp.sum((token_position[None, :] < token_position[:, None]).astype(jnp.int32), axis=1)
    local = token_position % row_count
    lane = jnp.arange(128, dtype=jnp.int32)[None, :]
    high, low = (local // 16)[:, None], (local % 16)[:, None]
    tail = jnp.where(lane == 0, high, jnp.where(lane == 1, low, 0)).astype(BF16)
    order = rank[None, :] == index[:, None]
    sent = select_rows(order, jnp.concatenate([features, tail], axis=1))
    arrived = lax.all_to_all(sent, "ep", split_axis=0, concat_axis=0, tiled=True)
    landing = (arrived[:, vis].astype(F32) * 16 + arrived[:, vis + 1].astype(F32)).astype(jnp.int32)
    patches = select_rows(landing[None, :] == index[:, None], arrived[:, :vis])

    pre_act = jnp.einsum("rk,gkn->rgn", patches, first_full, preferred_element_type=F32)
    pre_act = pre_act.reshape(row_count, width)
    hidden = jax.nn.gelu(pre_act + bias_in, approximate=False).astype(BF16)
    result = jnp.einsum("rk,gkn->rgn", hidden, second_full, preferred_element_type=F32)
    tokens = (result.reshape(row_count, width) + bias_out).astype(BF16)

    wide = tokens.astype(F32)
    scale = lax.rsqrt(jnp.mean(wide * wide, axis=-1, keepdims=True) + EPSILON)
    normed = (wide * scale * norm_gain).astype(BF16)
    experts = router.shape[1]
    top_count = expert_ids.shape[1]
    capacity = 2 * row_count * top_count // experts
    local_experts = w_gate.shape[0]
    logits = jnp.dot(normed, router, preferred_element_type=F32)
    numbers = jnp.arange(experts, dtype=jnp.int32)
    chosen_mask = expert_ids[:, :, None] == numbers[None, None, :]
    chosen = jnp.sum(jnp.where(chosen_mask, logits[:, None, :], 0.0), axis=2)
    first_gate = jax.nn.sigmoid(chosen[:, 0] - chosen[:, 1])
    gates = (first_gate, 1.0 - first_gate)

    named = jnp.any(chosen_mask, axis=1)
    earlier = (index[None, :] < index[:, None]).astype(BF16)
    before = jnp.dot(earlier, named.astype(BF16), preferred_element_type=F32).astype(jnp.int32)
    place = jnp.where(named, before, -1)
    slots = jnp.arange(capacity, dtype=jnp.int32)
    filled = place.T[:, None, :] == slots[None, :, None]
    blocks = select_rows(filled.reshape(experts * capacity, row_count), normed)
    blocks = blocks.reshape(members, local_experts, capacity, width)
    received = lax.all_to_all(blocks, "ep", split_axis=0, concat_axis=0, tiled=True)
    gate_part = jnp.einsum("pecd,edf->pecf", received, w_gate, preferred_element_type=F32)
    up_part = jnp.einsum("pecd,edf->pecf", received, w_up, preferred_element_type=F32)
    activated = (jax.nn.silu(gate_part) * up_part).astype(BF16)
    outputs = jnp.einsum("pecf,efd->pecd", activated, w_down, preferred_element_type=F32).astype(BF16)
    returned = lax.all_to_all(outputs, "ep", split_axis=0, concat_axis=0, tiled=True)
    returned = returned.reshape(experts * capacity, width)
    total = 0.0
    for choice in range(top_count):
        slot = jnp.where(chosen_mask[:, choice], before, -1)
        picked = (slot[:, :, None] == slots[None, None, :]).reshape(row_count, experts * capacity)
        row = jnp.dot(picked.astype(BF16), returned, preferred_element_type=F32)
        total = total + gates[choice][:, None] * row
    return (wide + total).astype(BF16)


def solution(mesh):
    placed = (
        P(("grp", "ep"), None),
        P(("grp", "ep")),
        P(("grp", "ep"), None),
        P("ep", None),
        P(),
        P("ep", None),
        P(),
        P(),
        P(),
        P("ep", None, None),
        P("ep", None, None),
        P("ep", None, None),
    )
    return jax.shard_map(
        shards, mesh=mesh, in_specs=placed, out_specs=P(("grp", "ep"), None), check_vma=False
    )
```

```python
import jax
import jax.numpy as jnp
from jax import lax
from jax.sharding import PartitionSpec as P

EPSILON = 1e-06
F32 = jnp.float32
BF16 = jnp.bfloat16
CHUNKS = 2


def select_rows(mask, rows):
    return jnp.dot(mask.astype(BF16), rows, preferred_element_type=F32).astype(BF16)


def gather_columns(weight):
    members = lax.axis_size("grp")
    width = weight.shape[1] // members
    part = lax.dynamic_slice_in_dim(weight, lax.axis_index("grp") * width, width, 1)
    full = lax.all_gather(part, ("grp", "ep"), axis=0, tiled=True)
    return full.reshape(members, -1, width)


def gather_rows(weight, column, width):
    depth = weight.shape[0] // lax.axis_size("grp")
    start = lax.axis_index("grp") * depth
    part = lax.dynamic_slice(weight, (start, column), (depth, width))
    return lax.all_gather(part, ("ep", "grp"), axis=0, tiled=True)


def shards(
    features,
    token_position,
    expert_ids,
    proj_in,
    bias_in,
    proj_out,
    bias_out,
    norm_gain,
    router,
    w_gate,
    w_up,
    w_down,
):
    members = lax.axis_size("ep")
    row_count, vis = features.shape
    width = proj_in.shape[1]
    step = width // CHUNKS
    columns = [slice(c * step, (c + 1) * step) for c in range(CHUNKS)]
    first_full = gather_columns(proj_in)
    second_full = [gather_rows(proj_out, c * step, step) for c in range(CHUNKS)]

    index = jnp.arange(row_count, dtype=jnp.int32)
    rank = jnp.sum((token_position[None, :] < token_position[:, None]).astype(jnp.int32), axis=1)
    local = token_position % row_count
    lane = jnp.arange(128, dtype=jnp.int32)[None, :]
    high, low = (local // 16)[:, None], (local % 16)[:, None]
    tail = jnp.where(lane == 0, high, jnp.where(lane == 1, low, 0)).astype(BF16)
    order = rank[None, :] == index[:, None]
    sent = select_rows(order, jnp.concatenate([features, tail], axis=1))
    arrived = lax.all_to_all(sent, "ep", split_axis=0, concat_axis=0, tiled=True)
    landing = (arrived[:, vis].astype(F32) * 16 + arrived[:, vis + 1].astype(F32)).astype(jnp.int32)
    patches = select_rows(landing[None, :] == index[:, None], arrived[:, :vis])

    parts = first_full.shape[0]
    pieces = []
    for g, bias in enumerate(jnp.split(bias_in, parts)):
        pre_act = jnp.dot(patches, first_full[g], preferred_element_type=F32)
        pieces.append(jax.nn.gelu(pre_act + bias, approximate=False).astype(BF16))
    hidden = jnp.concatenate(pieces, axis=1)

    experts = router.shape[1]
    top_count = expert_ids.shape[1]
    capacity = 2 * row_count * top_count // experts
    local_experts = w_gate.shape[0]
    numbers = jnp.arange(experts, dtype=jnp.int32)
    chosen_mask = expert_ids[:, :, None] == numbers[None, None, :]
    named = jnp.any(chosen_mask, axis=1)
    earlier = (index[None, :] < index[:, None]).astype(BF16)
    before = jnp.dot(earlier, named.astype(BF16), preferred_element_type=F32).astype(jnp.int32)
    place = jnp.where(named, before, -1)
    slots = jnp.arange(capacity, dtype=jnp.int32)
    filled = (place.T[:, None, :] == slots[None, :, None]).reshape(experts * capacity, row_count)
    filled = filled.astype(BF16)

    tokens, received = [], []
    for c, cols in enumerate(columns):
        result = jnp.dot(hidden, second_full[c], preferred_element_type=F32)
        part = (result + bias_out[cols]).astype(BF16)
        blocks = select_rows(filled, part).reshape(members, local_experts, capacity, step)
        tokens.append(part)
        received.append(lax.all_to_all(blocks, "ep", split_axis=0, concat_axis=0, tiled=True))

    def normed_parts(parts):
        wide = [part.astype(F32) for part in parts]
        square = sum(jnp.sum(part * part, axis=-1, keepdims=True) for part in wide)
        scale = lax.rsqrt(square / width + EPSILON)
        return [(part * scale * norm_gain[cols]).astype(BF16) for part, cols in zip(wide, columns)]

    normed = normed_parts(tokens)
    logits = sum(
        jnp.dot(part, router[cols], preferred_element_type=F32)
        for part, cols in zip(normed, columns)
    )
    chosen = jnp.sum(jnp.where(chosen_mask, logits[:, None, :], 0.0), axis=2)
    first_gate = jax.nn.sigmoid(chosen[:, 0] - chosen[:, 1])
    gates = (first_gate, 1.0 - first_gate)

    def expand(rows, weight):
        return sum(
            jnp.einsum("pecd,edf->pecf", part, weight[:, cols], preferred_element_type=F32)
            for part, cols in zip(rows, columns)
        )

    rows = normed_parts(received)
    activated = (jax.nn.silu(expand(rows, w_gate)) * expand(rows, w_up)).astype(BF16)
    picked = []
    for choice in range(top_count):
        slot = jnp.where(chosen_mask[:, choice], before, -1)
        picked.append((slot[:, :, None] == slots[None, None, :]).reshape(row_count, experts * capacity))
    mixed = []
    for part, cols in zip(tokens, columns):
        outputs = jnp.einsum(
            "pecf,efd->pecd", activated, w_down[:, :, cols], preferred_element_type=F32
        ).astype(BF16)
        returned = lax.all_to_all(outputs, "ep", split_axis=0, concat_axis=0, tiled=True)
        returned = returned.reshape(experts * capacity, step)
        total = 0.0
        for choice in range(top_count):
            row = jnp.dot(picked[choice].astype(BF16), returned, preferred_element_type=F32)
            total = total + gates[choice][:, None] * row
        mixed.append((part.astype(F32) + total).astype(BF16))
    return jnp.concatenate(mixed, axis=1)


def solution(mesh):
    placed = (
        P(("grp", "ep"), None),
        P(("grp", "ep")),
        P(("grp", "ep"), None),
        P("ep", None),
        P(),
        P("ep", None),
        P(),
        P(),
        P(),
        P("ep", None, None),
        P("ep", None, None),
        P("ep", None, None),
    )
    return jax.shard_map(
        shards, mesh=mesh, in_specs=placed, out_specs=P(("grp", "ep"), None), check_vma=False
    )
```

```python
import jax
import jax.numpy as jnp
from jax import lax
from jax.experimental import pallas as pl
from jax.experimental.pallas import tpu as pltpu
from jax.sharding import PartitionSpec as P

EPSILON = 1e-06
F32 = jnp.float32
BF16 = jnp.bfloat16


def select_rows(mask, rows):
    return jnp.dot(mask.astype(BF16), rows, preferred_element_type=F32).astype(BF16)


def gather_columns(*weights):
    members = lax.axis_size("grp")
    width = weights[0].shape[1] // members
    start = lax.axis_index("grp") * width
    parts = [lax.dynamic_slice_in_dim(weight, start, width, 1) for weight in weights]
    return lax.all_gather(jnp.concatenate(parts, axis=0), ("grp", "ep"), axis=0)


def weight_kernel(start, rows_ref, weight_ref, out_ref):
    blocks, _, depth = rows_ref.shape
    span = pl.ds(start, depth)

    def one(e):
        return jnp.dot(rows_ref[e], weight_ref[e, span, :], preferred_element_type=F32)

    if blocks <= 8:
        out_ref[...] = sum(one(e) for e in range(blocks))
    else:
        out_ref[...] = jnp.zeros_like(out_ref)

        @pl.loop(0, blocks)
        def _(e):
            out_ref[...] += one(e)


def weight_dot(rows, gathered, start, depth):
    blocks = lax.axis_size("ep")
    total, height, width = gathered.shape
    count = rows.shape[0]
    rows = rows.reshape(count, blocks, depth).swapaxes(0, 1)
    read = depth if start == 0 and depth % 16 == 0 else height
    parts = total // blocks
    return pl.pallas_call(
        lambda *refs: weight_kernel(start, *refs),
        grid=(parts,),
        in_specs=[
            pl.BlockSpec((blocks, count, depth), lambda g: (0, 0, 0)),
            pl.BlockSpec((blocks, read, width), lambda g: (g, 0, 0)),
        ],
        out_specs=pl.BlockSpec((count, width), lambda g: (0, g)),
        out_shape=jax.ShapeDtypeStruct((count, parts * width), F32),
        compiler_params=pltpu.CompilerParams(vmem_limit_bytes=40 << 20),
        cost_estimate=pl.CostEstimate(
            flops=2 * count * parts * blocks * depth * width,
            bytes_accessed=2 * parts * blocks * read * width,
            transcendentals=0,
        ),
    )(rows, gathered)


def shards(
    features,
    token_position,
    expert_ids,
    proj_in,
    bias_in,
    proj_out,
    bias_out,
    norm_gain,
    router,
    w_gate,
    w_up,
    w_down,
):
    members = lax.axis_size("ep")
    row_count, vis = features.shape
    width = proj_in.shape[1]
    gathered = gather_columns(proj_in, proj_out)
    depth = proj_in.shape[0]

    index = jnp.arange(row_count, dtype=jnp.int32)
    rank = jnp.sum((token_position[None, :] < token_position[:, None]).astype(jnp.int32), axis=1)
    local = token_position % row_count
    lane = jnp.arange(128, dtype=jnp.int32)[None, :]
    high, low = (local // 16)[:, None], (local % 16)[:, None]
    tail = jnp.where(lane == 0, high, jnp.where(lane == 1, low, 0)).astype(BF16)
    order = rank[None, :] == index[:, None]
    sent = select_rows(order, jnp.concatenate([features, tail], axis=1))
    arrived = lax.all_to_all(sent, "ep", split_axis=0, concat_axis=0, tiled=True)
    landing = (arrived[:, vis].astype(F32) * 16 + arrived[:, vis + 1].astype(F32)).astype(jnp.int32)
    patches = select_rows(landing[None, :] == index[:, None], arrived[:, :vis])

    pre_act = weight_dot(patches, gathered, 0, depth)
    hidden = jax.nn.gelu(pre_act + bias_in, approximate=False).astype(BF16)
    result = weight_dot(hidden, gathered, depth, proj_out.shape[0])
    tokens = (result + bias_out).astype(BF16)

    wide = tokens.astype(F32)
    scale = lax.rsqrt(jnp.mean(wide * wide, axis=-1, keepdims=True) + EPSILON)
    normed = (wide * scale * norm_gain).astype(BF16)
    experts = router.shape[1]
    top_count = expert_ids.shape[1]
    capacity = 2 * row_count * top_count // experts
    local_experts = w_gate.shape[0]
    logits = jnp.dot(normed, router, preferred_element_type=F32)
    numbers = jnp.arange(experts, dtype=jnp.int32)
    chosen_mask = expert_ids[:, :, None] == numbers[None, None, :]
    chosen = jnp.sum(jnp.where(chosen_mask, logits[:, None, :], 0.0), axis=2)
    first_gate = jax.nn.sigmoid(chosen[:, 0] - chosen[:, 1])
    gates = (first_gate, 1.0 - first_gate)

    named = jnp.any(chosen_mask, axis=1)
    earlier = (index[None, :] < index[:, None]).astype(BF16)
    before = jnp.dot(earlier, named.astype(BF16), preferred_element_type=F32).astype(jnp.int32)
    place = jnp.where(named, before, -1)
    slots = jnp.arange(capacity, dtype=jnp.int32)
    filled = place.T[:, None, :] == slots[None, :, None]
    blocks = select_rows(filled.reshape(experts * capacity, row_count), normed)
    blocks = blocks.reshape(members, local_experts, capacity, width)
    received = lax.all_to_all(blocks, "ep", split_axis=0, concat_axis=0, tiled=True)
    gate_part = jnp.einsum("pecd,edf->pecf", received, w_gate, preferred_element_type=F32)
    up_part = jnp.einsum("pecd,edf->pecf", received, w_up, preferred_element_type=F32)
    activated = (jax.nn.silu(gate_part) * up_part).astype(BF16)
    outputs = jnp.einsum("pecf,efd->pecd", activated, w_down, preferred_element_type=F32).astype(BF16)
    returned = lax.all_to_all(outputs, "ep", split_axis=0, concat_axis=0, tiled=True)
    returned = returned.reshape(experts * capacity, width)
    total = 0.0
    for choice in range(top_count):
        slot = jnp.where(chosen_mask[:, choice], before, -1)
        picked = (slot[:, :, None] == slots[None, None, :]).reshape(row_count, experts * capacity)
        row = jnp.dot(picked.astype(BF16), returned, preferred_element_type=F32)
        total = total + gates[choice][:, None] * row
    return (wide + total).astype(BF16)


def solution(mesh):
    placed = (
        P(("grp", "ep"), None),
        P(("grp", "ep")),
        P(("grp", "ep"), None),
        P("ep", None),
        P(),
        P("ep", None),
        P(),
        P(),
        P(),
        P("ep", None, None),
        P("ep", None, None),
        P("ep", None, None),
    )
    return jax.shard_map(
        shards, mesh=mesh, in_specs=placed, out_specs=P(("grp", "ep"), None), check_vma=False
    )
```

```python
import jax
import jax.numpy as jnp
from jax import lax
from jax.experimental import pallas as pl
from jax.experimental.pallas import tpu as pltpu
from jax.sharding import PartitionSpec as P

EPSILON = 1e-06
F32 = jnp.float32
BF16 = jnp.bfloat16


def select_rows(mask, rows):
    return jnp.dot(mask.astype(BF16), rows, preferred_element_type=F32).astype(BF16)


def gather_columns(*weights):
    members = lax.axis_size("grp")
    width = weights[0].shape[1] // members
    start = lax.axis_index("grp") * width
    parts = [lax.dynamic_slice_in_dim(weight, start, width, 1) for weight in weights]
    return lax.all_gather(jnp.concatenate(parts, axis=0), ("grp", "ep"), axis=0)


def weight_kernel(start, rows_ref, weight_ref, out_ref):
    blocks, _, depth = rows_ref.shape
    span = pl.ds(start, depth)

    def one(e):
        return jnp.dot(rows_ref[e], weight_ref[e, span, :], preferred_element_type=F32)

    if blocks <= 8:
        out_ref[...] = sum(one(e) for e in range(blocks))
    else:
        out_ref[...] = jnp.zeros_like(out_ref)

        @pl.loop(0, blocks)
        def _(e):
            out_ref[...] += one(e)


def weight_dot(rows, gathered, start, depth):
    blocks = lax.axis_size("ep")
    total, height, width = gathered.shape
    count = rows.shape[0]
    rows = rows.reshape(count, blocks, depth).swapaxes(0, 1)
    read = depth if start == 0 and depth % 16 == 0 else height
    parts = total // blocks
    return pl.pallas_call(
        lambda *refs: weight_kernel(start, *refs),
        grid=(parts,),
        in_specs=[
            pl.BlockSpec((blocks, count, depth), lambda g: (0, 0, 0)),
            pl.BlockSpec((blocks, read, width), lambda g: (g, 0, 0)),
        ],
        out_specs=pl.BlockSpec((count, width), lambda g: (0, g)),
        out_shape=jax.ShapeDtypeStruct((count, parts * width), F32),
        compiler_params=pltpu.CompilerParams(vmem_limit_bytes=40 << 20),
        cost_estimate=pl.CostEstimate(
            flops=2 * count * parts * blocks * depth * width,
            bytes_accessed=2 * parts * blocks * read * width,
            transcendentals=0,
        ),
    )(rows, gathered)


def shards(
    features,
    token_position,
    expert_ids,
    proj_in,
    bias_in,
    proj_out,
    bias_out,
    norm_gain,
    router,
    w_gate,
    w_up,
    w_down,
):
    members = lax.axis_size("ep")
    row_count, vis = features.shape
    width = proj_in.shape[1]
    gathered = gather_columns(proj_in, proj_out)
    depth = proj_in.shape[0]

    far = lax.axis_size("ep") // 2
    far_ids = lax.ppermute(expert_ids, "ep", [(i, (i + far) % members) for i in range(members)])
    index = jnp.arange(row_count, dtype=jnp.int32)
    rank = jnp.sum((token_position[None, :] < token_position[:, None]).astype(jnp.int32), axis=1)
    local = token_position % row_count
    lane = jnp.arange(128, dtype=jnp.int32)[None, :]
    high, low = (local // 16)[:, None], (local % 16)[:, None]
    tail = jnp.where(lane == 0, high, jnp.where(lane == 1, low, 0)).astype(BF16)
    order = rank[None, :] == index[:, None]
    sent = select_rows(order, jnp.concatenate([features, tail], axis=1))
    arrived = lax.all_to_all(sent, "ep", split_axis=0, concat_axis=0, tiled=True)
    landing = (arrived[:, vis].astype(F32) * 16 + arrived[:, vis + 1].astype(F32)).astype(jnp.int32)
    patches = select_rows(landing[None, :] == index[:, None], arrived[:, :vis])

    pre_act = weight_dot(patches, gathered, 0, depth)
    hidden = jax.nn.gelu(pre_act + bias_in, approximate=False).astype(BF16)
    result = weight_dot(hidden, gathered, depth, proj_out.shape[0])
    tokens = (result + bias_out).astype(BF16)

    wide = tokens.astype(F32)
    scale = lax.rsqrt(jnp.mean(wide * wide, axis=-1, keepdims=True) + EPSILON)
    normed = (wide * scale * norm_gain).astype(BF16)
    half = members // 2
    swap = [(i, (i + half) % members) for i in range(members)]
    groups = [list(range(half)), list(range(half, members))]
    experts = router.shape[1]
    near = experts // 2
    first_near = lax.axis_index("ep") // half * near
    top_count = expert_ids.shape[1]
    capacity = 2 * row_count * top_count // experts
    local_experts = w_gate.shape[0]
    numbers = jnp.arange(experts, dtype=jnp.int32)
    slots = jnp.arange(capacity, dtype=jnp.int32)
    earlier = (index[None, :] < index[:, None]).astype(BF16)

    def exchange(blocks):
        return lax.all_to_all(
            blocks, "ep", split_axis=0, concat_axis=0, axis_index_groups=groups, tiled=True
        )

    def plan(ids):
        chosen_mask = ids[:, :, None] == numbers[None, None, :]
        named = jnp.any(chosen_mask, axis=1)
        before = jnp.dot(earlier, named.astype(BF16), preferred_element_type=F32).astype(jnp.int32)
        return chosen_mask, named, before

    def dispatch(routes, rows):
        _, named, before = routes
        place = lax.dynamic_slice_in_dim(jnp.where(named, before, -1).T, first_near, near, 0)
        filled = place[:, None, :] == slots[None, :, None]
        blocks = select_rows(filled.reshape(near * capacity, row_count), rows)
        return exchange(blocks.reshape(half, local_experts, capacity, width))

    def run(received):
        gate_part = jnp.einsum("pecd,edf->pecf", received, w_gate, preferred_element_type=F32)
        up_part = jnp.einsum("pecd,edf->pecf", received, w_up, preferred_element_type=F32)
        activated = (jax.nn.silu(gate_part) * up_part).astype(BF16)
        outputs = jnp.einsum("pecf,efd->pecd", activated, w_down, preferred_element_type=F32)
        return exchange(outputs.astype(BF16)).reshape(near * capacity, width)

    def combine(routes, rows, returned):
        chosen_mask, _, before = routes
        logits = jnp.dot(rows, router, preferred_element_type=F32)
        chosen = jnp.sum(jnp.where(chosen_mask, logits[:, None, :], 0.0), axis=2)
        first_gate = jax.nn.sigmoid(chosen[:, 0] - chosen[:, 1])
        gates = (first_gate, 1.0 - first_gate)
        total = 0.0
        for choice in range(top_count):
            slot = jnp.where(chosen_mask[:, choice], before, -1)
            slot = lax.dynamic_slice_in_dim(slot, first_near, near, 1)
            picked = (slot[:, :, None] == slots[None, None, :]).reshape(row_count, near * capacity)
            row = jnp.dot(picked.astype(BF16), returned, preferred_element_type=F32)
            total = total + gates[choice][:, None] * row
        return total

    own_plan = plan(expert_ids)
    far_plan = plan(far_ids)
    far_rows = lax.ppermute(normed, "ep", swap)
    own_received = dispatch(own_plan, normed)
    far_rows, own_received = lax.optimization_barrier((far_rows, own_received))
    far_received = dispatch(far_plan, far_rows)
    far_total = combine(far_plan, far_rows, run(far_received)).astype(BF16)
    far_back = lax.ppermute(far_total, "ep", swap)
    total = combine(own_plan, normed, run(own_received))
    return (wide + total + far_back.astype(F32)).astype(BF16)


def solution(mesh):
    placed = (
        P(("grp", "ep"), None),
        P(("grp", "ep")),
        P(("grp", "ep"), None),
        P("ep", None),
        P(),
        P("ep", None),
        P(),
        P(),
        P(),
        P("ep", None, None),
        P("ep", None, None),
        P("ep", None, None),
    )
    return jax.shard_map(
        shards, mesh=mesh, in_specs=placed, out_specs=P(("grp", "ep"), None), check_vma=False
    )
```
